32 devices in a mesh: lat: 8 (over z, y), rep: 4 (over x, core).
Axes of the slice: x: 2, y: 2, z: 4, core: 2. Of those that a mesh axis runs over, the one named last changes fastest.
Arguments:
- legendre_table: bfloat16 [1024, 4, 8, 1025], P('lat', 'rep'), may hold values from -0.1875 to 0.1875
- fourier: bfloat16 [2, 1024, 4, 8, 2, 24], P(None, 'lat', None, None, None, 'rep'), may hold values from -6 to 6
- pair_low: int32 [4, 8], replicated, may hold values from 0 to 511
Outputs:
- spectral: float32 [4, 8, 1025, 24], P(None, 'lat', None, 'rep')
The draws below stay inside these ranges and needn't reach their ends.
Inputs may be any that keep to these rules, and one draw needn't show every extreme that they name: The pair slot holds the wavenumbers pair_low and 1023 - pair_low.
All inputs are finite; a program needn't handle non-finite values.
Results may differ from the reference program's by a relative error of at most 0.0031.
Values may be sent and summed in bfloat16 or wider, within the bound.
A program may use at most 64 MiB of HBM per device.

```python
import jax
import jax.numpy as jnp
from jax import lax

NLAT = 2048
TRUNC = 1024
PO = 4
NHALF = 1024
KP = 1025
OWNERS = 8
F2 = 24


def set_ends(result, rng, low, high):
    place = [jax.random.randint(jax.random.fold_in(rng, axis), (), 0, length) for axis, length in enumerate(result.shape)]
    main_axis = result.shape.index(max(result.shape))
    next_to = place[:main_axis] + [(place[main_axis] + 1) % result.shape[main_axis]] + place[main_axis + 1:]
    return result.at[tuple(place)].set(low).at[tuple(next_to)].set(high)


def spiked(result, own_key, source, target, blocks, factor):
    owner, partner = [(jnp.arange(result.shape[axis_at]) // (result.shape[axis_at] // blocks)).reshape([-1 if axis == axis_at else 1 for axis in range(result.ndim)]) for axis_at in (source, target)]
    chosen = jax.random.permutation(own_key, blocks)[partner]
    strong = (owner == chosen) | (owner == (partner + blocks // 2) % blocks)
    return jnp.where(strong, factor * result, result)


def levels(key, extent, cuts, smallest, high):
    factor_of, own = 1.0, jax.random.fold_in(key, 6)
    for dim, shards_of in cuts:
        draws = jnp.exp(jax.random.uniform(jax.random.fold_in(own, dim), (shards_of,), jnp.float32, smallest / len(cuts), high / len(cuts)))
        factor_of = factor_of * jnp.repeat(draws, extent[dim] // shards_of).reshape([-1 if axis == dim else 1 for axis in range(len(extent))])
    return factor_of


def scatter_about(rng, shape, deviation, most, pieces=(), kind=jnp.bfloat16):
    array = deviation * jax.random.normal(rng, shape, jnp.float32)
    if pieces:
        array = array * levels(rng, shape, pieces, -0.22, 0.18)
    return jnp.clip(array, -most, most).astype(kind)


def bell_draw_with(own_key, dims, deviation, limit, shards, heavy, kind=jnp.bfloat16):
    values = deviation * jax.random.normal(own_key, dims, jnp.float32)
    if shards:
        values = values * levels(own_key, dims, shards, -0.22, 0.18)
    return jnp.clip(spiked(values, jax.random.fold_in(own_key, 3), *heavy), -limit, limit).astype(kind)


def setup_inputs(seed: int = 0) -> dict:
    arg_keys = jax.random.split(jax.random.key(seed), 4)
    return {
        "legendre_table": bell_draw_with(arg_keys[0], (NHALF, PO, OWNERS, KP), NLAT ** -0.5, 0.1875, ((0, 8), (1, 4)), (0, 2, 8, 2.0)),
        "fourier": scatter_about(arg_keys[1], (2, NHALF, PO, OWNERS, 2, F2), 1.0, 6.0, ((1, 8), (5, 4))),
        "pair_low": set_ends(jax.random.randint(arg_keys[2], (PO, OWNERS), 0, TRUNC // 2), jax.random.fold_in(arg_keys[2], 1), 0, (TRUNC // 2) - 1).astype(jnp.int32),
    }


def selector(lows, width):
    column = jnp.arange(width, dtype=jnp.int32)
    split = (TRUNC - lows).astype(jnp.int32)[..., None]
    upper = column >= split
    offset = jnp.where(upper, column - split, column)
    index = 2 * upper.astype(jnp.int32) + offset % 2
    return index[..., None, :] == jnp.arange(4, dtype=jnp.int32)[:, None]


def combine(fourier):
    north = fourier[0].astype(jnp.float32)
    south = fourier[1].astype(jnp.float32)
    parts = [north[..., 0, :] + south[..., 0, :], north[..., 0, :] - south[..., 0, :],
             north[..., 1, :] + south[..., 1, :], north[..., 1, :] - south[..., 1, :]]
    return jnp.stack(parts, axis=-2).astype(jnp.bfloat16)


def reference(legendre_table, fourier, pair_low):
    combos = combine(fourier)
    chosen = selector(pair_low, legendre_table.shape[3]).astype(jnp.float32)

    def owner_sum(owner):
        table_one = lax.dynamic_index_in_dim(legendre_table, owner, axis=2, keepdims=False).astype(jnp.float32)
        combo_one = lax.dynamic_index_in_dim(combos, owner, axis=2, keepdims=False).astype(jnp.float32)
        mask_one = lax.dynamic_index_in_dim(chosen, owner, axis=1, keepdims=False)
        masked = table_one[:, :, None, :] * mask_one[None]
        return jnp.einsum('ljqc,ljqf->jcf', masked, combo_one, precision=lax.Precision.HIGHEST)

    blocks = lax.map(owner_sum, jnp.arange(legendre_table.shape[2], dtype=jnp.int32))
    return jnp.transpose(blocks, (1, 0, 2, 3))
```

```python
import functools

import jax
import jax.numpy as jnp
from jax import lax
from jax.experimental import pallas as pl
from jax.experimental.pallas import tpu as pltpu
from jax.sharding import PartitionSpec as P

MESH = pl.DeviceIdType.MESH
LANES = 128
SUB = 8


def selector(lows, width):
    column = jnp.arange(width, dtype=jnp.int32)
    split = (width - 1 - lows)[..., None]
    upper = column >= split
    offset = jnp.where(upper, column - split, column)
    index = 2 * upper.astype(jnp.int32) + offset % 2
    return index[..., None, :] == jnp.arange(4, dtype=jnp.int32)[:, None]


def combine(fourier):
    north = fourier[0].astype(jnp.float32)
    south = fourier[1].astype(jnp.float32)
    parts = [
        north[..., 0, :] + south[..., 0, :],
        north[..., 0, :] - south[..., 0, :],
        north[..., 1, :] + south[..., 1, :],
        north[..., 1, :] - south[..., 1, :],
    ]
    return jnp.stack(parts, axis=-2).astype(jnp.bfloat16)


def local_sums(table_blk, fourier_blk, lows_blk):
    combos = combine(fourier_blk)
    chosen = selector(lows_blk, table_blk.shape[3]).astype(jnp.bfloat16)
    masked = table_blk[:, :, :, None, :] * chosen[None]
    return jnp.einsum("ljoqc,ljoqf->jocf", masked, combos, preferred_element_type=jnp.float32)


def moved_table(legendre_table, fourier, pair_low):
    quarter = legendre_table.shape[1]
    lows_blk = lax.dynamic_slice_in_dim(pair_low, lax.axis_index("rep") * quarter, quarter, 0)
    lows_own = lax.dynamic_slice_in_dim(lows_blk, lax.axis_index("lat"), 1, 1)
    table_blk = lax.all_to_all(legendre_table, "lat", split_axis=2, concat_axis=0, tiled=True)
    fourier_blk = lax.all_to_all(
        lax.all_to_all(fourier, "lat", split_axis=3, concat_axis=1, tiled=True),
        "rep",
        split_axis=2,
        concat_axis=5,
        tiled=True,
    )
    owned = local_sums(table_blk, fourier_blk, lows_own)
    return lax.all_to_all(owned, "rep", split_axis=3, concat_axis=0, tiled=True)


def kernel(
    nlat, nrep, cols, trunc,
    low_ref, table_ref, mine_ref, out_ref,
    raw, wide, split, combos, block, outgoing, incoming, total,
    load_sem, give_sem, take_sem, send_sem, recv_sem,
):
    me_l, me_r = lax.axis_index("lat"), lax.axis_index("rep")
    tiles = trunc // LANES
    rows = LANES * nlat
    n = nlat * nrep
    me = me_l * nrep + me_r

    barrier = pltpu.get_barrier_semaphore()

    @pl.loop(1, n)
    def _(k):
        peer = lax.rem(me + k, n)
        pl.semaphore_signal(barrier, inc=1, device_id=(peer // nrep, lax.rem(peer, nrep)), device_id_type=MESH)

    def load(i, count):
        part = pl.ds(pl.multiple_of(i * rows, rows), count)
        return pltpu.make_async_copy(table_ref.at[part], raw.at[part], load_sem.at[i])

    @pl.loop(0, tiles)
    def _(i):
        load(i, rows).start()

    load(tiles, nlat).start()
    block[...] = jnp.zeros_like(block)
    combos[me_r] = mine_ref[me_r]

    pl.semaphore_wait(barrier, n - 1)

    def give(k):
        other = lax.rem(me_r + k, nrep)
        return pltpu.make_async_remote_copy(
            src_ref=mine_ref.at[other],
            dst_ref=combos.at[me_r],
            send_sem=give_sem.at[other],
            recv_sem=take_sem.at[me_r],
            device_id=(me_l, other),
            device_id_type=MESH,
        )

    def take(k):
        other = lax.rem(me_r + k, nrep)
        return pltpu.make_async_remote_copy(
            src_ref=mine_ref.at[other],
            dst_ref=combos.at[other],
            send_sem=give_sem.at[other],
            recv_sem=take_sem.at[other],
            device_id=(me_l, other),
            device_id_type=MESH,
        )

    for k in range(1, nrep):
        give(k).start()

    @pl.loop(0, tiles)
    def _(i):
        load(i, rows).wait()
        wide[...] = raw[pl.ds(pl.multiple_of(i * rows, rows), rows), :].astype(jnp.float32)
        for o in range(nlat):
            split[o, pl.ds(pl.multiple_of(i * LANES, LANES), LANES), :] = wide[pl.ds(o, LANES, stride=nlat), :].astype(jnp.bfloat16)

    load(tiles, nlat).wait()
    last = raw[rows * tiles:, :].astype(jnp.float32)
    for o in range(nlat):
        split[o, tiles * LANES:, :] = jnp.broadcast_to(last[o:o + 1], (LANES, LANES)).astype(jnp.bfloat16)

    for k in range(1, nrep):
        take(k).wait_recv()

    def send(o, r):
        return pltpu.make_async_remote_copy(
            src_ref=outgoing.at[o, r],
            dst_ref=incoming.at[me_l, me_r],
            send_sem=send_sem.at[o, r],
            recv_sem=recv_sem.at[me_l, me_r],
            device_id=(o, r),
            device_id_type=MESH,
        )

    lane = lax.broadcasted_iota(jnp.int32, (SUB, LANES), 1)

    @pl.loop(0, nlat)
    def _(k):
        o = lax.rem(me_l + nlat // 2 + k, nlat)
        edge = trunc - low_ref[me_r, o]
        left = jnp.concatenate([combos[r, o] for r in range(nrep)], axis=0)
        for t in range(tiles + 1):
            got = lax.dot_general(
                left, split[o, t * LANES:(t + 1) * LANES, :], (((1,), (1,)), ((), ())),
                preferred_element_type=jnp.float32,
            )
            column = lane + t * LANES if t < tiles else jnp.full_like(lane, trunc)
            upper = column >= edge
            odd = (jnp.where(upper, column - edge, column) & 1) == 1
            for r in range(nrep):
                q = [got[(4 * r + s) * SUB:(4 * r + s + 1) * SUB] for s in range(4)]
                value = jnp.where(upper, jnp.where(odd, q[3], q[2]), jnp.where(odd, q[1], q[0]))
                block[r, t * cols:(t + 1) * cols, :] = value[:cols]
        for r in range(nrep):
            outgoing[o, r] = block[r].astype(jnp.bfloat16)
        for r in range(nrep):
            @pl.when(jnp.logical_or(o != me_l, r != me_r))
            def _():
                send(o, r).start()

    incoming[me_l, me_r] = outgoing[me_l, me_r]

    def receive(l, r):
        return pltpu.make_async_remote_copy(
            src_ref=outgoing.at[l, r],
            dst_ref=incoming.at[l, r],
            send_sem=send_sem.at[l, r],
            recv_sem=recv_sem.at[l, r],
            device_id=(l, r),
            device_id_type=MESH,
        )

    @pl.loop(0, nrep)
    def _(j):
        for l in range(nlat):
            @pl.when(jnp.logical_or(l != me_l, j != me_r))
            def _():
                receive(l, j).wait_recv()
        acc = incoming[0, j].astype(jnp.float32)
        for l in range(1, nlat):
            acc = acc + incoming[l, j].astype(jnp.float32)
        total[...] = acc
        for t in range(tiles):
            out_ref[j, :, t * LANES:(t + 1) * LANES] = total[t * cols:(t + 1) * cols, :]
        out_ref[j, :, tiles * LANES:] = total[tiles * cols:(tiles + 1) * cols, 0:1]

    for k in range(1, nrep):
        give(k).wait_send()

    @pl.loop(1, n)
    def _(k):
        peer = lax.rem(me + k, n)
        send(peer // nrep, lax.rem(peer, nrep)).wait_send()


def kept_table(nlat, nrep, legendre_table, fourier, pair_low):
    lats, _, owners, width = legendre_table.shape
    slots, cols = fourier.shape[2], fourier.shape[5]
    trunc = width - 1
    table = jnp.transpose(legendre_table[:, 0], (2, 1, 0)).reshape(width * owners, lats)
    mine = jnp.transpose(combine(fourier), (1, 2, 3, 4, 0))
    mine = jnp.pad(mine, ((0, 0), (0, 0), (0, 0), (0, SUB - cols), (0, 0)))
    mine = mine.reshape(slots, owners, 4 * SUB, lats)
    tiles = trunc // LANES
    height = -(-(tiles + 1) * cols // SUB) * SUB
    bf16, f32 = jnp.bfloat16, jnp.float32
    vmem = pl.BlockSpec(memory_space=pltpu.VMEM)
    out = pl.pallas_call(
        functools.partial(kernel, nlat, nrep, cols, trunc),
        out_shape=jax.ShapeDtypeStruct((slots, cols, width), f32),
        in_specs=[pl.BlockSpec(memory_space=pltpu.SMEM), pl.BlockSpec(memory_space=pl.ANY), vmem],
        out_specs=vmem,
        scratch_shapes=[
            pltpu.VMEM((width * owners, lats), bf16),
            pltpu.VMEM((LANES * owners, lats), f32),
            pltpu.VMEM((owners, trunc + LANES, lats), bf16),
            pltpu.VMEM((nrep, owners, 4 * SUB, lats), bf16),
            pltpu.VMEM((nrep, height, LANES), f32),
            pltpu.VMEM((nlat, nrep, height, LANES), bf16),
            pltpu.VMEM((nlat, nrep, height, LANES), bf16),
            pltpu.VMEM((height, LANES), f32),
            pltpu.SemaphoreType.DMA((tiles + 1,)),
            pltpu.SemaphoreType.DMA((nrep,)),
            pltpu.SemaphoreType.DMA((nrep,)),
            pltpu.SemaphoreType.DMA((nlat, nrep)),
            pltpu.SemaphoreType.DMA((nlat, nrep)),
        ],
        compiler_params=pltpu.CompilerParams(collective_id=0, has_side_effects=True),
        cost_estimate=pl.CostEstimate(
            flops=2 * 4 * nrep * SUB * lats * owners * (trunc + LANES),
            bytes_accessed=2 * width * owners * lats,
            transcendentals=0,
        ),
    )(pair_low, table, mine)
    return jnp.transpose(out, (0, 2, 1))[:, None]


def solution(mesh):
    nlat, nrep = mesh.shape["lat"], mesh.shape["rep"]

    def per_device(legendre_table, fourier, pair_low):
        lats, quarter, owners, width = legendre_table.shape
        fits = (
            lats == LANES
            and quarter == 1
            and owners == nlat
            and nlat == SUB
            and fourier.shape[2] == nrep
            and fourier.shape[5] <= SUB
            and (width - 1) % LANES == 0
        )
        if fits:
            return kept_table(nlat, nrep, legendre_table, fourier, pair_low)
        return moved_table(legendre_table, fourier, pair_low)

    return jax.shard_map(
        per_device,
        mesh=mesh,
        in_specs=(P("lat", "rep", None, None), P(None, "lat", None, None, None, "rep"), P()),
        out_specs=P(None, "lat", None, "rep"),
        check_vma=False,
    )
```

```python
import functools

import jax
import jax.numpy as jnp
from jax import lax
from jax.experimental import pallas as pl
from jax.experimental.pallas import tpu as pltpu
from jax.sharding import PartitionSpec as P

MESH = pl.DeviceIdType.MESH
LANES = 128
SUB = 8


def selector(lows, width):
    column = jnp.arange(width, dtype=jnp.int32)
    split = (width - 1 - lows)[..., None]
    upper = column >= split
    offset = jnp.where(upper, column - split, column)
    index = 2 * upper.astype(jnp.int32) + offset % 2
    return index[..., None, :] == jnp.arange(4, dtype=jnp.int32)[:, None]


def combine(fourier):
    north = fourier[0].astype(jnp.float32)
    south = fourier[1].astype(jnp.float32)
    parts = [
        north[..., 0, :] + south[..., 0, :],
        north[..., 0, :] - south[..., 0, :],
        north[..., 1, :] + south[..., 1, :],
        north[..., 1, :] - south[..., 1, :],
    ]
    return jnp.stack(parts, axis=-2).astype(jnp.bfloat16)


def local_sums(table_blk, fourier_blk, lows_blk):
    combos = combine(fourier_blk)
    chosen = selector(lows_blk, table_blk.shape[3]).astype(jnp.bfloat16)
    masked = table_blk[:, :, :, None, :] * chosen[None]
    return jnp.einsum("ljoqc,ljoqf->jocf", masked, combos, preferred_element_type=jnp.float32)


def moved_table(legendre_table, fourier, pair_low):
    quarter = legendre_table.shape[1]
    lows_blk = lax.dynamic_slice_in_dim(pair_low, lax.axis_index("rep") * quarter, quarter, 0)
    lows_own = lax.dynamic_slice_in_dim(lows_blk, lax.axis_index("lat"), 1, 1)
    table_blk = lax.all_to_all(legendre_table, "lat", split_axis=2, concat_axis=0, tiled=True)
    fourier_blk = lax.all_to_all(
        lax.all_to_all(fourier, "lat", split_axis=3, concat_axis=1, tiled=True),
        "rep",
        split_axis=2,
        concat_axis=5,
        tiled=True,
    )
    owned = local_sums(table_blk, fourier_blk, lows_own)
    return lax.all_to_all(owned, "rep", split_axis=3, concat_axis=0, tiled=True)


def kernel(
    nlat, nrep, cols, trunc,
    low_hbm, table_ref, four_hbm, out_ref,
    low_ref, four_ref, raw, wide, split, mine, combos, block, outgoing, incoming, total,
    low_sem, four_sem, load_sem, give_sem, take_sem, send_sem, recv_sem,
):
    me_l, me_r = lax.axis_index("lat"), lax.axis_index("rep")
    tiles = trunc // LANES
    rows = LANES * nlat
    n = nlat * nrep
    me = me_l * nrep + me_r

    barrier = pltpu.get_barrier_semaphore()
    get_four = pltpu.make_async_copy(four_hbm, four_ref, four_sem)
    get_low = pltpu.make_async_copy(low_hbm, low_ref, low_sem)
    get_four.start()
    get_low.start()

    @pl.loop(1, n)
    def _(k):
        peer = lax.rem(me + k, n)
        pl.semaphore_signal(barrier, inc=1, device_id=(peer // nrep, lax.rem(peer, nrep)), device_id_type=MESH)

    def load(i, count):
        part = pl.ds(pl.multiple_of(i * rows, rows), count)
        return pltpu.make_async_copy(table_ref.at[part], raw.at[part], load_sem.at[i])

    @pl.loop(0, tiles)
    def _(i):
        load(i, rows).start()

    load(tiles, nlat).start()
    block[...] = jnp.zeros_like(block)

    pairs = four_ref.shape[2]
    to = lax.broadcasted_iota(jnp.int32, (nlat * 4 * SUB, pairs), 0)
    frm = lax.broadcasted_iota(jnp.int32, (nlat * 4 * SUB, pairs), 1)
    o_to, q_to, f_to = to // (4 * SUB), lax.rem(to // SUB, 4), lax.rem(to, SUB)
    hit = (f_to < cols) & (frm == (o_to * cols + f_to) * 2 + q_to // 2)
    north = jnp.where(hit, 1.0, 0.0).astype(jnp.bfloat16)
    south = jnp.where(hit, jnp.where(lax.rem(q_to, 2) == 1, -1.0, 1.0), 0.0).astype(jnp.bfloat16)
    get_four.wait()
    get_low.wait()
    for r in range(nrep):
        both = jnp.dot(north, four_ref[0, r], preferred_element_type=jnp.float32)
        both = both + jnp.dot(south, four_ref[1, r], preferred_element_type=jnp.float32)
        mine[r] = both.astype(jnp.bfloat16).reshape(nlat, 4 * SUB, LANES)
    combos[me_r] = mine[me_r]

    pl.semaphore_wait(barrier, n - 1)

    def give(k):
        other = lax.rem(me_r + k, nrep)
        return pltpu.make_async_remote_copy(
            src_ref=mine.at[other],
            dst_ref=combos.at[me_r],
            send_sem=give_sem.at[other],
            recv_sem=take_sem.at[me_r],
            device_id=(me_l, other),
            device_id_type=MESH,
        )

    def take(k):
        other = lax.rem(me_r + k, nrep)
        return pltpu.make_async_remote_copy(
            src_ref=mine.at[other],
            dst_ref=combos.at[other],
            send_sem=give_sem.at[other],
            recv_sem=take_sem.at[other],
            device_id=(me_l, other),
            device_id_type=MESH,
        )

    for k in range(1, nrep):
        give(k).start()

    @pl.loop(0, tiles)
    def _(i):
        load(i, rows).wait()
        wide[...] = raw[pl.ds(pl.multiple_of(i * rows, rows), rows), :].astype(jnp.float32)
        for o in range(nlat):
            split[o, pl.ds(pl.multiple_of(i * LANES, LANES), LANES), :] = wide[pl.ds(o, LANES, stride=nlat), :].astype(jnp.bfloat16)

    load(tiles, nlat).wait()
    last = raw[rows * tiles:, :].astype(jnp.float32)
    for o in range(nlat):
        split[o, tiles * LANES:, :] = jnp.broadcast_to(last[o:o + 1], (LANES, LANES)).astype(jnp.bfloat16)

    for k in range(1, nrep):
        take(k).wait_recv()

    def send(o, r):
        return pltpu.make_async_remote_copy(
            src_ref=outgoing.at[o, r],
            dst_ref=incoming.at[me_l, me_r],
            send_sem=send_sem.at[o, r],
            recv_sem=recv_sem.at[me_l, me_r],
            device_id=(o, r),
            device_id_type=MESH,
        )

    lane = lax.broadcasted_iota(jnp.int32, (SUB, LANES), 1)
    row = lax.broadcasted_iota(jnp.int32, (SUB, LANES), 0)

    @pl.loop(0, nlat)
    def _(k):
        o = lax.rem(me_l + nlat // 2 + k, nlat)
        edge = trunc - low_ref[me_r, o]
        left = jnp.concatenate([combos[r, o] for r in range(nrep)], axis=0)
        for t in range(tiles + 1):
            got = lax.dot_general(
                left, split[o, t * LANES:(t + 1) * LANES, :], (((1,), (1,)), ((), ())),
                preferred_element_type=jnp.float32,
            )
            column = lane + t * LANES if t < tiles else jnp.full_like(lane, trunc)
            upper = column >= edge
            odd = (jnp.where(upper, column - edge, column) & 1) == 1
            for r in range(nrep):
                q = [got[(4 * r + s) * SUB:(4 * r + s + 1) * SUB] for s in range(4)]
                value = jnp.where(upper, jnp.where(odd, q[3], q[2]), jnp.where(odd, q[1], q[0]))
                if t < tiles:
                    block[r, t * cols:(t + 1) * cols, :] = value[:cols]
                else:
                    block[r, t * cols:t * cols + 1, :] = jnp.sum(jnp.where(lane == row, value, 0.0), axis=0, keepdims=True)
        for r in range(nrep):
            outgoing[o, r] = block[r].astype(jnp.bfloat16)
        for r in range(nrep):
            @pl.when(jnp.logical_or(o != me_l, r != me_r))
            def _():
                send(o, r).start()

    incoming[me_l, me_r] = outgoing[me_l, me_r]

    def receive(l, r):
        return pltpu.make_async_remote_copy(
            src_ref=outgoing.at[l, r],
            dst_ref=incoming.at[l, r],
            send_sem=send_sem.at[l, r],
            recv_sem=recv_sem.at[l, r],
            device_id=(l, r),
            device_id_type=MESH,
        )

    @pl.loop(0, nrep)
    def _(j):
        for l in range(nlat):
            @pl.when(jnp.logical_or(l != me_l, j != me_r))
            def _():
                receive(l, j).wait_recv()
        acc = incoming[0, j].astype(jnp.float32)
        for l in range(1, nlat):
            acc = acc + incoming[l, j].astype(jnp.float32)
        total[...] = acc
        for t in range(tiles):
            out_ref[j, :, 0, t * LANES:(t + 1) * LANES] = total[t * cols:(t + 1) * cols, :]
        ends = jnp.broadcast_to(total[tiles * cols:tiles * cols + 1, :], (SUB, LANES))
        ends = jnp.sum(jnp.where(lane == row, ends, 0.0), axis=1, keepdims=True)
        out_ref[j, :, 0, tiles * LANES:] = ends[:cols]

    for k in range(1, nrep):
        give(k).wait_send()

    @pl.loop(1, n)
    def _(k):
        peer = lax.rem(me + k, n)
        send(peer // nrep, lax.rem(peer, nrep)).wait_send()


def kept_table(nlat, nrep, legendre_table, fourier, pair_low):
    lats, _, owners, width = legendre_table.shape
    slots, cols = fourier.shape[2], fourier.shape[5]
    trunc = width - 1
    table = jnp.transpose(legendre_table[:, 0], (2, 1, 0)).reshape(width * owners, lats)
    columns = jnp.transpose(fourier, (0, 2, 3, 5, 4, 1)).reshape(2, slots, owners * cols * 2, lats)
    tiles = trunc // LANES
    height = tiles * cols + 2
    bf16, f32 = jnp.bfloat16, jnp.float32
    vmem = pl.BlockSpec(memory_space=pltpu.VMEM)
    out = pl.pallas_call(
        functools.partial(kernel, nlat, nrep, cols, trunc),
        out_shape=jax.ShapeDtypeStruct((slots, cols, 1, width), f32),
        in_specs=[pl.BlockSpec(memory_space=pltpu.HBM)] * 3,
        out_specs=vmem,
        scratch_shapes=[
            pltpu.SMEM(pair_low.shape, jnp.int32),
            pltpu.VMEM(columns.shape, bf16),
            pltpu.VMEM((width * owners, lats), bf16),
            pltpu.VMEM((LANES * owners, lats), f32),
            pltpu.VMEM((owners, trunc + LANES, lats), bf16),
            pltpu.VMEM((nrep, owners, 4 * SUB, lats), bf16),
            pltpu.VMEM((nrep, owners, 4 * SUB, lats), bf16),
            pltpu.VMEM((nrep, height, LANES), f32),
            pltpu.VMEM((nlat, nrep, height, LANES), bf16),
            pltpu.VMEM((nlat, nrep, height, LANES), bf16),
            pltpu.VMEM((height, LANES), f32),
            pltpu.SemaphoreType.DMA,
            pltpu.SemaphoreType.DMA,
            pltpu.SemaphoreType.DMA((tiles + 1,)),
            pltpu.SemaphoreType.DMA((nrep,)),
            pltpu.SemaphoreType.DMA((nrep,)),
            pltpu.SemaphoreType.DMA((nlat, nrep)),
            pltpu.SemaphoreType.DMA((nlat, nrep)),
        ],
        compiler_params=pltpu.CompilerParams(collective_id=0, has_side_effects=True, vmem_limit_bytes=55000 << 10),
        cost_estimate=pl.CostEstimate(
            flops=2 * 4 * nrep * SUB * lats * owners * (trunc + LANES),
            bytes_accessed=2 * width * owners * lats,
            transcendentals=0,
        ),
    )(pair_low, table, columns)
    return jnp.transpose(out, (0, 2, 3, 1))


def solution(mesh):
    nlat, nrep = mesh.shape["lat"], mesh.shape["rep"]

    def per_device(legendre_table, fourier, pair_low):
        lats, quarter, owners, width = legendre_table.shape
        fits = (
            lats == LANES
            and quarter == 1
            and owners == nlat
            and nlat == SUB
            and fourier.shape[2] == nrep
            and fourier.shape[5] <= SUB
            and (width - 1) % LANES == 0
        )
        if fits:
            return kept_table(nlat, nrep, legendre_table, fourier, pair_low)
        return moved_table(legendre_table, fourier, pair_low)

    return jax.shard_map(
        per_device,
        mesh=mesh,
        in_specs=(P("lat", "rep", None, None), P(None, "lat", None, None, None, "rep"), P()),
        out_specs=P(None, "lat", None, "rep"),
        check_vma=False,
    )
```

```python
import functools

import jax
import jax.numpy as jnp
from jax import lax
from jax.experimental import pallas as pl
from jax.experimental.pallas import tpu as pltpu
from jax.sharding import PartitionSpec as P

MESH = pl.DeviceIdType.MESH
LANES = 128
SUB = 8


def selector(lows, width):
    column = jnp.arange(width, dtype=jnp.int32)
    split = (width - 1 - lows)[..., None]
    upper = column >= split
    offset = jnp.where(upper, column - split, column)
    index = 2 * upper.astype(jnp.int32) + offset % 2
    return index[..., None, :] == jnp.arange(4, dtype=jnp.int32)[:, None]


def combine(fourier):
    north = fourier[0].astype(jnp.float32)
    south = fourier[1].astype(jnp.float32)
    parts = [
        north[..., 0, :] + south[..., 0, :],
        north[..., 0, :] - south[..., 0, :],
        north[..., 1, :] + south[..., 1, :],
        north[..., 1, :] - south[..., 1, :],
    ]
    return jnp.stack(parts, axis=-2).astype(jnp.bfloat16)


def local_sums(table_blk, fourier_blk, lows_blk):
    combos = combine(fourier_blk)
    chosen = selector(lows_blk, table_blk.shape[3]).astype(jnp.bfloat16)
    masked = table_blk[:, :, :, None, :] * chosen[None]
    return jnp.einsum("ljoqc,ljoqf->jocf", masked, combos, preferred_element_type=jnp.float32)


def moved_table(legendre_table, fourier, pair_low):
    quarter = legendre_table.shape[1]
    lows_blk = lax.dynamic_slice_in_dim(pair_low, lax.axis_index("rep") * quarter, quarter, 0)
    lows_own = lax.dynamic_slice_in_dim(lows_blk, lax.axis_index("lat"), 1, 1)
    table_blk = lax.all_to_all(legendre_table, "lat", split_axis=2, concat_axis=0, tiled=True)
    fourier_blk = lax.all_to_all(
        lax.all_to_all(fourier, "lat", split_axis=3, concat_axis=1, tiled=True),
        "rep",
        split_axis=2,
        concat_axis=5,
        tiled=True,
    )
    owned = local_sums(table_blk, fourier_blk, lows_own)
    return lax.all_to_all(owned, "rep", split_axis=3, concat_axis=0, tiled=True)


def kernel(
    nlat, nrep, cols, trunc,
    low_hbm, table_ref, four_hbm, out_ref,
    low_ref, four_ref, raw, wide, split, mine, combos, block, outgoing, incoming, total,
    low_sem, four_sem, load_sem, give_sem, take_sem, send_sem, recv_sem,
):
    me_l, me_r = lax.axis_index("lat"), lax.axis_index("rep")
    tiles = trunc // LANES
    rows = LANES * nlat
    n = nlat * nrep
    me = me_l * nrep + me_r

    barrier = pltpu.get_barrier_semaphore()
    get_four = pltpu.make_async_copy(four_hbm, four_ref, four_sem)
    get_low = pltpu.make_async_copy(low_hbm, low_ref, low_sem)
    get_four.start()
    get_low.start()

    @pl.loop(1, n)
    def _(k):
        peer = lax.rem(me + k, n)
        pl.semaphore_signal(barrier, inc=1, device_id=(peer // nrep, lax.rem(peer, nrep)), device_id_type=MESH)

    def load(i, count):
        part = pl.ds(pl.multiple_of(i * rows, rows), count)
        return pltpu.make_async_copy(table_ref.at[part], raw.at[part], load_sem.at[i])

    @pl.loop(0, tiles)
    def _(i):
        load(i, rows).start()

    load(tiles, nlat).start()
    block[...] = jnp.zeros_like(block)

    pairs = four_ref.shape[2]
    to = lax.broadcasted_iota(jnp.int32, (nlat * 4 * SUB, pairs), 0)
    frm = lax.broadcasted_iota(jnp.int32, (nlat * 4 * SUB, pairs), 1)
    o_to, q_to, f_to = to // (4 * SUB), lax.rem(to // SUB, 4), lax.rem(to, SUB)
    hit = (f_to < cols) & (frm == (o_to * cols + f_to) * 2 + q_to // 2)
    north = jnp.where(hit, 1.0, 0.0).astype(jnp.bfloat16)
    south = jnp.where(hit, jnp.where(lax.rem(q_to, 2) == 1, -1.0, 1.0), 0.0).astype(jnp.bfloat16)
    get_four.wait()
    get_low.wait()
    for r in range(nrep):
        both = jnp.dot(north, four_ref[0, r], preferred_element_type=jnp.float32)
        both = both + jnp.dot(south, four_ref[1, r], preferred_element_type=jnp.float32)
        mine[r] = both.astype(jnp.bfloat16).reshape(nlat, 4 * SUB, LANES)
    combos[me_r] = mine[me_r]

    pl.semaphore_wait(barrier, n - 1)

    def give(k):
        other = lax.rem(me_r + k, nrep)
        return pltpu.make_async_remote_copy(
            src_ref=mine.at[other],
            dst_ref=combos.at[me_r],
            send_sem=give_sem.at[other],
            recv_sem=take_sem.at[me_r],
            device_id=(me_l, other),
            device_id_type=MESH,
        )

    def take(k):
        other = lax.rem(me_r + k, nrep)
        return pltpu.make_async_remote_copy(
            src_ref=mine.at[other],
            dst_ref=combos.at[other],
            send_sem=give_sem.at[other],
            recv_sem=take_sem.at[other],
            device_id=(me_l, other),
            device_id_type=MESH,
        )

    for k in range(1, nrep):
        give(k).start()

    @pl.loop(0, tiles)
    def _(i):
        load(i, rows).wait()
        wide[...] = raw[pl.ds(pl.multiple_of(i * rows, rows), rows), :].astype(jnp.float32)
        for o in range(nlat):
            split[o, pl.ds(pl.multiple_of(i * LANES, LANES), LANES), :] = wide[pl.ds(o, LANES, stride=nlat), :].astype(jnp.bfloat16)

    load(tiles, nlat).wait()
    last = raw[rows * tiles:, :].astype(jnp.float32)
    for o in range(nlat):
        split[o, tiles * LANES:, :] = jnp.broadcast_to(last[o:o + 1], (LANES, LANES)).astype(jnp.bfloat16)

    def send(o, r):
        return pltpu.make_async_remote_copy(
            src_ref=outgoing.at[o, r],
            dst_ref=incoming.at[me_l, me_r],
            send_sem=send_sem.at[o, r],
            recv_sem=recv_sem.at[me_l, me_r],
            device_id=(o, r),
            device_id_type=MESH,
        )

    lane = lax.broadcasted_iota(jnp.int32, (SUB, LANES), 1)
    row = lax.broadcasted_iota(jnp.int32, (SUB, LANES), 0)
    half = nlat // 2

    def far_first(k):
        return lax.rem(1 - me_l // half + k // half, 2) * half + lax.rem(me_l + k, half)

    def partial_sums(o, groups):
        edge = trunc - low_ref[me_r, o]
        left = jnp.concatenate([combos[r, o] for r in groups], axis=0)
        for t in range(tiles + 1):
            got = lax.dot_general(
                left, split[o, t * LANES:(t + 1) * LANES, :], (((1,), (1,)), ((), ())),
                preferred_element_type=jnp.float32,
            )
            column = lane + t * LANES if t < tiles else jnp.full_like(lane, trunc)
            upper = column >= edge
            odd = (jnp.where(upper, column - edge, column) & 1) == 1
            for i in range(len(groups)):
                q = [got[(4 * i + s) * SUB:(4 * i + s + 1) * SUB] for s in range(4)]
                value = jnp.where(upper, jnp.where(odd, q[3], q[2]), jnp.where(odd, q[1], q[0]))
                if t < tiles:
                    block[i, t * cols:(t + 1) * cols, :] = value[:cols]
                else:
                    block[i, t * cols:t * cols + 1, :] = jnp.sum(jnp.where(lane == row, value, 0.0), axis=0, keepdims=True)
        for i, r in enumerate(groups):
            outgoing[o, r] = block[i].astype(jnp.bfloat16)

    @pl.loop(0, nlat)
    def _(k):
        o = far_first(k)
        partial_sums(o, [me_r])

        @pl.when(o != me_l)
        def _():
            send(o, me_r).start()

    for k in range(1, nrep):
        take(k).wait_recv()

    @pl.loop(0, nlat)
    def _(k):
        o = far_first(k)
        others = [lax.rem(me_r + i, nrep) for i in range(1, nrep)]
        partial_sums(o, others)
        for r in others:
            send(o, r).start()

    incoming[me_l, me_r] = outgoing[me_l, me_r]

    def receive(l, r):
        return pltpu.make_async_remote_copy(
            src_ref=outgoing.at[l, r],
            dst_ref=incoming.at[l, r],
            send_sem=send_sem.at[l, r],
            recv_sem=recv_sem.at[l, r],
            device_id=(l, r),
            device_id_type=MESH,
        )

    @pl.loop(0, nrep)
    def _(j):
        for l in range(nlat):
            @pl.when(jnp.logical_or(l != me_l, j != me_r))
            def _():
                receive(l, j).wait_recv()
        acc = incoming[0, j].astype(jnp.float32)
        for l in range(1, nlat):
            acc = acc + incoming[l, j].astype(jnp.float32)
        total[...] = acc
        for t in range(tiles):
            out_ref[j, :, 0, t * LANES:(t + 1) * LANES] = total[t * cols:(t + 1) * cols, :]
        ends = jnp.broadcast_to(total[tiles * cols:tiles * cols + 1, :], (SUB, LANES))
        ends = jnp.sum(jnp.where(lane == row, ends, 0.0), axis=1, keepdims=True)
        out_ref[j, :, 0, tiles * LANES:] = ends[:cols]

    for k in range(1, nrep):
        give(k).wait_send()

    @pl.loop(1, n)
    def _(k):
        peer = lax.rem(me + k, n)
        send(peer // nrep, lax.rem(peer, nrep)).wait_send()


def kept_table(nlat, nrep, legendre_table, fourier, pair_low):
    lats, _, owners, width = legendre_table.shape
    slots, cols = fourier.shape[2], fourier.shape[5]
    trunc = width - 1
    table = jnp.transpose(legendre_table[:, 0], (2, 1, 0)).reshape(width * owners, lats)
    columns = jnp.transpose(fourier, (0, 2, 3, 5, 4, 1)).reshape(2, slots, owners * cols * 2, lats)
    tiles = trunc // LANES
    height = tiles * cols + 2
    bf16, f32 = jnp.bfloat16, jnp.float32
    vmem = pl.BlockSpec(memory_space=pltpu.VMEM)
    out = pl.pallas_call(
        functools.partial(kernel, nlat, nrep, cols, trunc),
        out_shape=jax.ShapeDtypeStruct((slots, cols, 1, width), f32),
        in_specs=[pl.BlockSpec(memory_space=pltpu.HBM)] * 3,
        out_specs=vmem,
        scratch_shapes=[
            pltpu.SMEM(pair_low.shape, jnp.int32),
            pltpu.VMEM(columns.shape, bf16),
            pltpu.VMEM((width * owners, lats), bf16),
            pltpu.VMEM((LANES * owners, lats), f32),
            pltpu.VMEM((owners, trunc + LANES, lats), bf16),
            pltpu.VMEM((nrep, owners, 4 * SUB, lats), bf16),
            pltpu.VMEM((nrep, owners, 4 * SUB, lats), bf16),
            pltpu.VMEM((nrep, height, LANES), f32),
            pltpu.VMEM((nlat, nrep, height, LANES), bf16),
            pltpu.VMEM((nlat, nrep, height, LANES), bf16),
            pltpu.VMEM((height, LANES), f32),
            pltpu.SemaphoreType.DMA,
            pltpu.SemaphoreType.DMA,
            pltpu.SemaphoreType.DMA((tiles + 1,)),
            pltpu.SemaphoreType.DMA((nrep,)),
            pltpu.SemaphoreType.DMA((nrep,)),
            pltpu.SemaphoreType.DMA((nlat, nrep)),
            pltpu.SemaphoreType.DMA((nlat, nrep)),
        ],
        compiler_params=pltpu.CompilerParams(collective_id=0, has_side_effects=True, vmem_limit_bytes=55000 << 10),
        cost_estimate=pl.CostEstimate(
            flops=2 * 4 * nrep * SUB * lats * owners * (trunc + LANES),
            bytes_accessed=2 * width * owners * lats,
            transcendentals=0,
        ),
    )(pair_low, table, columns)
    return jnp.transpose(out, (0, 2, 3, 1))


def solution(mesh):
    nlat, nrep = mesh.shape["lat"], mesh.shape["rep"]

    def per_device(legendre_table, fourier, pair_low):
        lats, quarter, owners, width = legendre_table.shape
        fits = (
            lats == LANES
            and quarter == 1
            and owners == nlat
            and nlat == SUB
            and fourier.shape[2] == nrep
            and fourier.shape[5] <= SUB
            and (width - 1) % LANES == 0
        )
        if fits:
            return kept_table(nlat, nrep, legendre_table, fourier, pair_low)
        return moved_table(legendre_table, fourier, pair_low)

    return jax.shard_map(
        per_device,
        mesh=mesh,
        in_specs=(P("lat", "rep", None, None), P(None, "lat", None, None, None, "rep"), P()),
        out_specs=P(None, "lat", None, "rep"),
        check_vma=False,
    )
```

```python
import functools

import jax
import jax.numpy as jnp
from jax import lax
from jax.experimental import pallas as pl
from jax.experimental.pallas import tpu as pltpu
from jax.sharding import PartitionSpec as P

MESH = pl.DeviceIdType.MESH
LANES = 128
SUB = 8


def selector(lows, width):
    column = jnp.arange(width, dtype=jnp.int32)
    split = (width - 1 - lows)[..., None]
    upper = column >= split
    offset = jnp.where(upper, column - split, column)
    index = 2 * upper.astype(jnp.int32) + offset % 2
    return index[..., None, :] == jnp.arange(4, dtype=jnp.int32)[:, None]


def combine(fourier):
    north = fourier[0].astype(jnp.float32)
    south = fourier[1].astype(jnp.float32)
    parts = [
        north[..., 0, :] + south[..., 0, :],
        north[..., 0, :] - south[..., 0, :],
        north[..., 1, :] + south[..., 1, :],
        north[..., 1, :] - south[..., 1, :],
    ]
    return jnp.stack(parts, axis=-2).astype(jnp.bfloat16)


def local_sums(table_blk, fourier_blk, lows_blk):
    combos = combine(fourier_blk)
    chosen = selector(lows_blk, table_blk.shape[3]).astype(jnp.bfloat16)
    masked = table_blk[:, :, :, None, :] * chosen[None]
    return jnp.einsum("ljoqc,ljoqf->jocf", masked, combos, preferred_element_type=jnp.float32)


def moved_table(legendre_table, fourier, pair_low):
    quarter = legendre_table.shape[1]
    lows_blk = lax.dynamic_slice_in_dim(pair_low, lax.axis_index("rep") * quarter, quarter, 0)
    lows_own = lax.dynamic_slice_in_dim(lows_blk, lax.axis_index("lat"), 1, 1)
    table_blk = lax.all_to_all(legendre_table, "lat", split_axis=2, concat_axis=0, tiled=True)
    fourier_blk = lax.all_to_all(
        lax.all_to_all(fourier, "lat", split_axis=3, concat_axis=1, tiled=True),
        "rep",
        split_axis=2,
        concat_axis=5,
        tiled=True,
    )
    owned = local_sums(table_blk, fourier_blk, lows_own)
    return lax.all_to_all(owned, "rep", split_axis=3, concat_axis=0, tiled=True)


def kernel(
    nlat, nrep, cols, trunc,
    low_hbm, table_ref, four_hbm, out_ref,
    low_ref, four_ref, raw, wide, split, mine, combos, block, outgoing, incoming, met, total,
    low_sem, four_sem, load_sem, give_sem, take_sem, send_sem, recv_sem, met_sem,
):
    me_l, me_r = lax.axis_index("lat"), lax.axis_index("rep")
    tiles = trunc // LANES
    rows = LANES * nlat
    n = nlat * nrep
    me = me_l * nrep + me_r

    barrier = pltpu.get_barrier_semaphore()
    get_four = pltpu.make_async_copy(four_hbm, four_ref, four_sem)
    get_low = pltpu.make_async_copy(low_hbm, low_ref, low_sem)
    get_four.start()
    get_low.start()

    @pl.loop(1, n)
    def _(k):
        peer = lax.rem(me + k, n)
        pl.semaphore_signal(barrier, inc=1, device_id=(peer // nrep, lax.rem(peer, nrep)), device_id_type=MESH)

    def load(i, count):
        part = pl.ds(pl.multiple_of(i * rows, rows), count)
        return pltpu.make_async_copy(table_ref.at[part], raw.at[part], load_sem.at[i])

    @pl.loop(0, tiles)
    def _(i):
        load(i, rows).start()

    load(tiles, nlat).start()
    block[...] = jnp.zeros_like(block)

    pairs = four_ref.shape[2]
    to = lax.broadcasted_iota(jnp.int32, (nlat * 4 * SUB, pairs), 0)
    frm = lax.broadcasted_iota(jnp.int32, (nlat * 4 * SUB, pairs), 1)
    o_to, q_to, f_to = to // (4 * SUB), lax.rem(to // SUB, 4), lax.rem(to, SUB)
    hit = (f_to < cols) & (frm == (o_to * cols + f_to) * 2 + q_to // 2)
    north = jnp.where(hit, 1.0, 0.0).astype(jnp.bfloat16)
    south = jnp.where(hit, jnp.where(lax.rem(q_to, 2) == 1, -1.0, 1.0), 0.0).astype(jnp.bfloat16)
    get_four.wait()
    get_low.wait()
    for r in range(nrep):
        both = jnp.dot(north, four_ref[0, r], preferred_element_type=jnp.float32)
        both = both + jnp.dot(south, four_ref[1, r], preferred_element_type=jnp.float32)
        mine[r] = both.astype(jnp.bfloat16).reshape(nlat, 4 * SUB, LANES)
    combos[me_r] = mine[me_r]

    pl.semaphore_wait(barrier, n - 1)

    def give(k):
        other = lax.rem(me_r + k, nrep)
        return pltpu.make_async_remote_copy(
            src_ref=mine.at[other],
            dst_ref=combos.at[me_r],
            send_sem=give_sem.at[other],
            recv_sem=take_sem.at[me_r],
            device_id=(me_l, other),
            device_id_type=MESH,
        )

    def take(k):
        other = lax.rem(me_r + k, nrep)
        return pltpu.make_async_remote_copy(
            src_ref=mine.at[other],
            dst_ref=combos.at[other],
            send_sem=give_sem.at[other],
            recv_sem=take_sem.at[other],
            device_id=(me_l, other),
            device_id_type=MESH,
        )

    for k in range(1, nrep):
        give(k).start()

    @pl.loop(0, tiles)
    def _(i):
        load(i, rows).wait()
        wide[...] = raw[pl.ds(pl.multiple_of(i * rows, rows), rows), :].astype(jnp.float32)
        for o in range(nlat):
            split[o, pl.ds(pl.multiple_of(i * LANES, LANES), LANES), :] = wide[pl.ds(o, LANES, stride=nlat), :].astype(jnp.bfloat16)

    load(tiles, nlat).wait()
    last = raw[rows * tiles:, :].astype(jnp.float32)
    for o in range(nlat):
        split[o, tiles * LANES:, :] = jnp.broadcast_to(last[o:o + 1], (LANES, LANES)).astype(jnp.bfloat16)

    def send(o, r):
        return pltpu.make_async_remote_copy(
            src_ref=outgoing.at[o, r],
            dst_ref=incoming.at[me_l, me_r],
            send_sem=send_sem.at[o, r],
            recv_sem=recv_sem.at[me_l, me_r],
            device_id=(o, r),
            device_id_type=MESH,
        )

    lane = lax.broadcasted_iota(jnp.int32, (SUB, LANES), 1)
    row = lax.broadcasted_iota(jnp.int32, (SUB, LANES), 0)
    half = nlat // 2

    side, parity = me_l // half, lax.rem(me_l, 2)
    partner = me_l + 1 - 2 * parity

    def near(k):
        return side * half + lax.rem(me_l + k, half)

    def far(i, which):
        return (1 - side) * half + 2 * i + which

    def hand(i, r):
        return pltpu.make_async_remote_copy(
            src_ref=outgoing.at[far(i, 1 - parity), r],
            dst_ref=met.at[i, r],
            send_sem=send_sem.at[far(i, 1 - parity), r],
            recv_sem=met_sem.at[i, r],
            device_id=(partner, me_r),
            device_id_type=MESH,
        )

    def partial_sums(o, groups, i_met=None):
        edge = trunc - low_ref[me_r, o]
        left = jnp.concatenate([combos[r, o] for r in groups], axis=0)
        for t in range(tiles + 1):
            got = lax.dot_general(
                left, split[o, t * LANES:(t + 1) * LANES, :], (((1,), (1,)), ((), ())),
                preferred_element_type=jnp.float32,
            )
            column = lane + t * LANES if t < tiles else jnp.full_like(lane, trunc)
            upper = column >= edge
            odd = (jnp.where(upper, column - edge, column) & 1) == 1
            for i in range(len(groups)):
                q = [got[(4 * i + s) * SUB:(4 * i + s + 1) * SUB] for s in range(4)]
                value = jnp.where(upper, jnp.where(odd, q[3], q[2]), jnp.where(odd, q[1], q[0]))
                if t < tiles:
                    block[i, t * cols:(t + 1) * cols, :] = value[:cols]
                else:
                    block[i, t * cols:t * cols + 1, :] = jnp.sum(jnp.where(lane == row, value, 0.0), axis=0, keepdims=True)
        for i, r in enumerate(groups):
            if i_met is None:
                outgoing[o, r] = block[i].astype(jnp.bfloat16)
            else:
                hand(i_met, r).wait_recv()
                outgoing[o, r] = (block[i] + met[i_met, r].astype(jnp.float32)).astype(jnp.bfloat16)

    def blocks(groups):
        @pl.loop(0, half // 2)
        def _(k):
            i = lax.rem(me_l // 2 + k, half // 2)
            partial_sums(far(i, 1 - parity), groups)
            for r in groups:
                hand(i, r).start()

        @pl.loop(0, half)
        def _(k):
            o = near(k)
            partial_sums(o, groups)
            for r in groups:
                @pl.when(jnp.logical_or(o != me_l, r != me_r))
                def _():
                    send(o, r).start()

        @pl.loop(0, half // 2)
        def _(k):
            i = lax.rem(me_l // 2 + k, half // 2)
            partial_sums(far(i, parity), groups, i)
            for r in groups:
                send(far(i, parity), r).start()

    blocks([me_r])
    for k in range(1, nrep):
        take(k).wait_recv()
    blocks([lax.rem(me_r + i, nrep) for i in range(1, nrep)])

    incoming[me_l, me_r] = outgoing[me_l, me_r]

    def receive(l, r):
        return pltpu.make_async_remote_copy(
            src_ref=outgoing.at[l, r],
            dst_ref=incoming.at[l, r],
            send_sem=send_sem.at[l, r],
            recv_sem=recv_sem.at[l, r],
            device_id=(l, r),
            device_id_type=MESH,
        )

    @pl.loop(0, nrep)
    def _(j):
        sources = [side * half + i for i in range(half)] + [far(i, parity) for i in range(half // 2)]
        acc = jnp.zeros(total.shape, jnp.float32)
        for l in sources:
            @pl.when(jnp.logical_or(l != me_l, j != me_r))
            def _():
                receive(l, j).wait_recv()
            acc = acc + incoming[l, j].astype(jnp.float32)
        total[...] = acc
        for t in range(tiles):
            out_ref[j, :, 0, t * LANES:(t + 1) * LANES] = total[t * cols:(t + 1) * cols, :]
        ends = jnp.broadcast_to(total[tiles * cols:tiles * cols + 1, :], (SUB, LANES))
        ends = jnp.sum(jnp.where(lane == row, ends, 0.0), axis=1, keepdims=True)
        out_ref[j, :, 0, tiles * LANES:] = ends[:cols]

    for k in range(1, nrep):
        give(k).wait_send()

    @pl.loop(1, n)
    def _(k):
        peer = lax.rem(me + k, n)
        send(peer // nrep, lax.rem(peer, nrep)).wait_send()


def kept_table(nlat, nrep, legendre_table, fourier, pair_low):
    lats, _, owners, width = legendre_table.shape
    slots, cols = fourier.shape[2], fourier.shape[5]
    trunc = width - 1
    table = jnp.transpose(legendre_table[:, 0], (2, 1, 0)).reshape(width * owners, lats)
    columns = jnp.transpose(fourier, (0, 2, 3, 5, 4, 1)).reshape(2, slots, owners * cols * 2, lats)
    tiles = trunc // LANES
    height = tiles * cols + 2
    bf16, f32 = jnp.bfloat16, jnp.float32
    vmem = pl.BlockSpec(memory_space=pltpu.VMEM)
    out = pl.pallas_call(
        functools.partial(kernel, nlat, nrep, cols, trunc),
        out_shape=jax.ShapeDtypeStruct((slots, cols, 1, width), f32),
        in_specs=[pl.BlockSpec(memory_space=pltpu.HBM)] * 3,
        out_specs=vmem,
        scratch_shapes=[
            pltpu.SMEM(pair_low.shape, jnp.int32),
            pltpu.VMEM(columns.shape, bf16),
            pltpu.VMEM((width * owners, lats), bf16),
            pltpu.VMEM((LANES * owners, lats), f32),
            pltpu.VMEM((owners, trunc + LANES, lats), bf16),
            pltpu.VMEM((nrep, owners, 4 * SUB, lats), bf16),
            pltpu.VMEM((nrep, owners, 4 * SUB, lats), bf16),
            pltpu.VMEM((nrep, height, LANES), f32),
            pltpu.VMEM((nlat, nrep, height, LANES), bf16),
            pltpu.VMEM((nlat, nrep, height, LANES), bf16),
            pltpu.VMEM((nlat // 4, nrep, height, LANES), bf16),
            pltpu.VMEM((height, LANES), f32),
            pltpu.SemaphoreType.DMA,
            pltpu.SemaphoreType.DMA,
            pltpu.SemaphoreType.DMA((tiles + 1,)),
            pltpu.SemaphoreType.DMA((nrep,)),
            pltpu.SemaphoreType.DMA((nrep,)),
            pltpu.SemaphoreType.DMA((nlat, nrep)),
            pltpu.SemaphoreType.DMA((nlat, nrep)),
            pltpu.SemaphoreType.DMA((nlat // 4, nrep)),
        ],
        compiler_params=pltpu.CompilerParams(collective_id=0, has_side_effects=True, vmem_limit_bytes=55000 << 10),
        cost_estimate=pl.CostEstimate(
            flops=2 * 4 * nrep * SUB * lats * owners * (trunc + LANES),
            bytes_accessed=2 * width * owners * lats,
            transcendentals=0,
        ),
    )(pair_low, table, columns)
    return jnp.transpose(out, (0, 2, 3, 1))


def solution(mesh):
    nlat, nrep = mesh.shape["lat"], mesh.shape["rep"]

    def per_device(legendre_table, fourier, pair_low):
        lats, quarter, owners, width = legendre_table.shape
        fits = (
            lats == LANES
            and quarter == 1
            and owners == nlat
            and nlat == SUB
            and fourier.shape[2] == nrep
            and fourier.shape[5] <= SUB
            and (width - 1) % LANES == 0
        )
        if fits:
            return kept_table(nlat, nrep, legendre_table, fourier, pair_low)
        return moved_table(legendre_table, fourier, pair_low)

    return jax.shard_map(
        per_device,
        mesh=mesh,
        in_specs=(P("lat", "rep", None, None), P(None, "lat", None, None, None, "rep"), P()),
        out_specs=P(None, "lat", None, "rep"),
        check_vma=False,
    )
```
